32 devices in a mesh: heads: 2 (over x), blk: 16 (over z, y, core).
Axes of the slice: x: 2, y: 2, z: 4, core: 2. Of those that a mesh axis runs over, the one named last changes fastest.
Arguments:
- queries: bfloat16 [1024, 64, 128], P('blk', 'heads'), may hold values from -8 to 8
- prefix_keys: bfloat16 [8, 32768, 128], P('heads', 'blk'), may hold values from -8 to 8
- cached_prefix_values: bfloat16 [8, 32768, 128], P('heads', 'blk'), may hold values from -6 to 6
- shard_len: int32 [16], replicated, may hold values from 512 to 2048
- reach: int32 [16], replicated, may hold values from 4096 to 8192
- w_out: bfloat16 [8192, 16384], P('heads', 'blk'), may hold values from -0.0625 to 0.0625
Outputs:
- projected: bfloat16 [1024, 16384], P('heads', 'blk')
The draws below stay inside these ranges and needn't reach their ends.
All inputs are finite; a program needn't handle non-finite values.
Results may differ from the reference program's by a relative error of at most 0.0056.
Values may be sent and summed in bfloat16 or wider, within the bound.
A program may use at most 128 MiB of HBM per device.

```python
import jax
import jax.numpy as jnp
from jax import lax

D = 16384
QUERY_HEADS = 64
KEY_VALUE_HEADS = 8
HEAD_DIM = 128
QUERY_TOKENS = 64
KEYS_DEV = 2048
SPAN = 4
SHARDS = 16
TOKENS = 1024
PREFIX_SLOTS = 32768


def draw_queries(key, part):
    random_seed_key = jax.random.fold_in(key, 1)
    random_sample = jnp.clip(jax.random.normal(random_seed_key, (TOKENS, QUERY_HEADS, HEAD_DIM), jnp.float32), -6.0, 6.0)
    return random_sample.astype(jnp.bfloat16)


def draw_prefix_keys(key, part):
    random_seed_key = jax.random.fold_in(key, 2)
    random_sample = jnp.clip(jax.random.normal(random_seed_key, (KEY_VALUE_HEADS, PREFIX_SLOTS, HEAD_DIM), jnp.float32), -6.0, 6.0)
    return random_sample.astype(jnp.bfloat16)


def with_ends(values, stream_key, smallest, high):
    longest = values.shape.index(max(values.shape))
    spots = []
    for shift in (0, 1):
        where = [jax.random.randint(jax.random.fold_in(stream_key, axis), (), 0, length) for axis, length in enumerate(values.shape)]
        where[longest] = (where[longest] + shift) % values.shape[longest]
        spots.append(tuple(where))
    return values.at[spots[0]].set(smallest).at[spots[1]].set(high)


def steps_of(key, shape, cuts, low, top_value):
    gain, own = 1.0, jax.random.fold_in(key, 6)
    for axis_at, parts in cuts:
        draws = jnp.exp(jax.random.uniform(jax.random.fold_in(own, axis_at), (parts,), jnp.float32, low / len(cuts), top_value / len(cuts)))
        gain = gain * jnp.repeat(draws, shape[axis_at] // parts).reshape([-1 if axis == axis_at else 1 for axis in range(len(shape))])
    return gain


def scatter_about(key, dims, width, most, shards=(), kind=jnp.bfloat16):
    loudness = steps_of(key, dims, shards, -0.22, 0.18) if shards else 1.0
    values = jax.random.normal(key, dims, jnp.float32) * width * loudness
    return jnp.minimum(jnp.maximum(values, -most), most).astype(kind)


def setup_inputs(seed: int = 0) -> dict:
    splits = jax.random.split(jax.random.key(seed), 7)
    queries = draw_queries(jax.random.fold_in(splits[6], 71), 0)
    prefix_keys = draw_prefix_keys(jax.random.fold_in(splits[6], 71), 0)
    cached_prefix_values = scatter_about(splits[2], (KEY_VALUE_HEADS, PREFIX_SLOTS, HEAD_DIM), 1.0, 6.0, ((0, 2), (1, 16)))
    shard_len = with_ends(jax.random.randint(splits[3], (SHARDS,), KEYS_DEV // 4, KEYS_DEV + 1), jax.random.fold_in(splits[3], 1), KEYS_DEV // 4, KEYS_DEV).astype(jnp.int32)
    reach = with_ends(jax.random.randint(splits[4], (SHARDS,), SPAN * KEYS_DEV // 2, SPAN * KEYS_DEV + 1), jax.random.fold_in(splits[4], 1), SPAN * KEYS_DEV // 2, SPAN * KEYS_DEV).astype(jnp.int32)
    w_out = scatter_about(splits[5], (QUERY_HEADS * HEAD_DIM, D), (QUERY_HEADS * HEAD_DIM) ** -0.5, 0.0625, ((0, 2), (1, 16)))
    return {"queries": queries, "prefix_keys": prefix_keys, "cached_prefix_values": cached_prefix_values, "shard_len": shard_len, "reach": reach, "w_out": w_out}


masked_score = -1e30


def part_stats(query_tile_rows, key_block, value_block, visible):
    scores = jnp.einsum("thgd,hnd->thgn", query_tile_rows.astype(jnp.float32), key_block.astype(jnp.float32)) * (HEAD_DIM ** -0.5)
    visible_grid = visible[:, None, None, :]
    maxima = jnp.max(jnp.where(visible_grid, scores, masked_score), axis=-1)
    weights = jnp.where(visible_grid, jnp.exp(scores - maxima[..., None]), 0.0)
    totals = jnp.sum(weights, axis=-1)
    weighted = jnp.einsum("thgn,hnd->thgd", weights.astype(jnp.bfloat16).astype(jnp.float32), value_block.astype(jnp.float32))
    return maxima, totals, weighted


def combine_parts(first, second):
    joined = jnp.maximum(first[0], second[0])
    first_factor = jnp.exp(first[0] - joined)
    second_factor = jnp.exp(second[0] - joined)
    totals = first[1] * first_factor + second[1] * second_factor
    weighted = first[2] * first_factor[..., None] + second[2] * second_factor[..., None]
    return joined, totals, weighted


def reference(queries, prefix_keys, cached_prefix_values, shard_len, reach, w_out):
    heads_per_group = QUERY_HEADS // KEY_VALUE_HEADS
    row_ids = jnp.arange(QUERY_TOKENS, dtype=jnp.int32)[:, None]
    slot_ids = jnp.arange(KEYS_DEV, dtype=jnp.int32)[None, :]

    def block_attention(block_id):
        starting_row = (block_id * QUERY_TOKENS).astype(jnp.int32)
        query_tile_rows = lax.dynamic_slice_in_dim(queries, starting_row, QUERY_TOKENS, 0).reshape(QUERY_TOKENS, KEY_VALUE_HEADS, heads_per_group, HEAD_DIM)
        running = None
        for offset in range(SPAN):
            shard_id = ((block_id + offset) % SHARDS).astype(jnp.int32)
            first_slot = (shard_id * KEYS_DEV).astype(jnp.int32)
            key_block = lax.dynamic_slice_in_dim(prefix_keys, first_slot, KEYS_DEV, 1)
            value_block = lax.dynamic_slice_in_dim(cached_prefix_values, first_slot, KEYS_DEV, 1)
            visible = (slot_ids < shard_len[shard_id]) & (offset * KEYS_DEV + slot_ids < reach[block_id] + row_ids)
            partial_value = part_stats(query_tile_rows, key_block, value_block, visible)
            running = partial_value if offset == 0 else combine_parts(running, partial_value)
        attended = (running[2] / running[1][..., None]).astype(jnp.bfloat16)
        return attended.reshape(QUERY_TOKENS, QUERY_HEADS * HEAD_DIM)

    attended = lax.map(block_attention, jnp.arange(SHARDS, dtype=jnp.int32)).reshape(TOKENS, QUERY_HEADS * HEAD_DIM)
    return jnp.dot(attended, w_out, preferred_element_type=jnp.float32).astype(jnp.bfloat16)
```

```python
import functools
import math

import jax
import jax.numpy as jnp
from jax import lax
from jax.experimental import pallas as pl
from jax.experimental.pallas import tpu as pltpu
from jax.sharding import PartitionSpec as P

SPAN = 4
LANES = 128
masked_score = -1e30


def passed_along(value, axis, steps):
    count = lax.axis_size(axis)
    pairs = [(source, (source + steps) % count) for source in range(count)]
    return lax.ppermute(value, axis, pairs)


def attend_kernel(tile, group, head_size, bounds, q_ref, k_ref, v_ref, o_ref, s_ref, q_all, m_ref, l_ref, acc_ref):
    rows = q_ref.shape[0]
    keys = k_ref.shape[1]
    kv = pl.program_id(0)
    live, edge = bounds[0], bounds[1]
    factor = head_size**-0.5 * math.log2(math.e)
    for g in range(group):
        q_all[g * rows : (g + 1) * rows, :] = q_ref[:, g * head_size : (g + 1) * head_size]
    m_ref[...] = jnp.full(m_ref.shape, masked_score, jnp.float32)
    l_ref[...] = jnp.zeros(l_ref.shape, jnp.float32)
    acc_ref[...] = jnp.zeros(acc_ref.shape, jnp.float32)

    def step(start, masked):
        k = k_ref[0, start : start + tile, :]
        v = v_ref[0, start : start + tile, :]
        s = lax.dot_general(
            q_all[...], k, (((1,), (1,)), ((), ())), preferred_element_type=jnp.float32
        ) * factor
        if masked:
            token = lax.broadcasted_iota(jnp.int32, (rows, tile), 0)
            slot = lax.broadcasted_iota(jnp.int32, (rows, tile), 1) + start
            seen = (slot < live) & (slot < edge + token)
            seen = jnp.concatenate([seen] * group, axis=0)
            s = jnp.where(seen, s, masked_score)
        m_old = m_ref[:, :1]
        m_new = jnp.maximum(m_old, jnp.max(s, axis=1, keepdims=True))
        p = jnp.exp2(s - m_new)
        if masked:
            p = jnp.where(seen, p, 0.0)
        shrink = jnp.exp2(m_old - m_new)
        l_new = l_ref[:, :1] * shrink + jnp.sum(p, axis=1, keepdims=True)
        acc_ref[...] = acc_ref[...] * shrink + jnp.dot(
            p.astype(jnp.bfloat16), v, preferred_element_type=jnp.float32
        )
        m_ref[...] = jnp.broadcast_to(m_new, m_ref.shape)
        l_ref[...] = jnp.broadcast_to(l_new, l_ref.shape)

    for start in range(0, keys, tile):
        whole = (start + tile <= live) & (start + tile <= edge)
        some = (start < live) & (start < edge + rows - 1)

        @pl.when(whole)
        def _():
            step(start, False)

        @pl.when(some & jnp.logical_not(whole))
        def _():
            step(start, True)

    total = l_ref[:, :1]
    held = jnp.where(total > 0.0, total, 1.0)
    out = acc_ref[...] / held
    stat = jnp.where(total > 0.0, m_ref[:, :1] + jnp.log2(held), masked_score)

    @pl.when(kv == 0)
    def _():
        s_ref[...] = jnp.full(s_ref.shape, masked_score, jnp.float32)

    lane = lax.broadcasted_iota(jnp.int32, s_ref.shape, 1)
    stats = s_ref[...]
    for g in range(group):
        o_ref[:, g * head_size : (g + 1) * head_size] = out[g * rows : (g + 1) * rows].astype(o_ref.dtype)
        stats = jnp.where(lane == kv * group + g, stat[g * rows : (g + 1) * rows], stats)
    s_ref[...] = stats


def attend(q, keys, values, bounds, group, tile):
    rows, width = q.shape
    kv_local, key_count, head_size = keys.shape
    wide = group * head_size
    return pl.pallas_call(
        functools.partial(attend_kernel, tile, group, head_size),
        out_shape=(
            jax.ShapeDtypeStruct((rows, width), jnp.bfloat16),
            jax.ShapeDtypeStruct((rows, LANES), jnp.float32),
        ),
        grid_spec=pltpu.PrefetchScalarGridSpec(
            num_scalar_prefetch=1,
            grid=(kv_local,),
            in_specs=[
                pl.BlockSpec((rows, wide), lambda i, b: (0, i)),
                pl.BlockSpec((1, key_count, head_size), lambda i, b: (i, 0, 0)),
                pl.BlockSpec((1, key_count, head_size), lambda i, b: (i, 0, 0)),
            ],
            out_specs=[
                pl.BlockSpec((rows, wide), lambda i, b: (0, i)),
                pl.BlockSpec((rows, LANES), lambda i, b: (0, 0)),
            ],
            scratch_shapes=[
                pltpu.VMEM((group * rows, head_size), jnp.bfloat16),
                pltpu.VMEM((group * rows, LANES), jnp.float32),
                pltpu.VMEM((group * rows, LANES), jnp.float32),
                pltpu.VMEM((group * rows, head_size), jnp.float32),
            ],
        ),
        compiler_params=pltpu.CompilerParams(vmem_limit_bytes=48 << 20),
        cost_estimate=pl.CostEstimate(
            flops=4 * rows * width * key_count,
            bytes_accessed=4 * rows * width + 4 * keys.size,
            transcendentals=rows * (width // head_size) * key_count,
        ),
    )(bounds, q, keys, values)


def merge_kernel(head_size, *refs):
    parts = len(refs) // 2
    outs, stats, final = refs[:parts], refs[parts : 2 * parts], refs[-1]
    joined = functools.reduce(jnp.maximum, [s[...] for s in stats])
    weights = [jnp.exp2(s[...] - joined) for s in stats]
    inverse = 1.0 / functools.reduce(jnp.add, weights)
    weights = [w * inverse for w in weights]
    for h in range(final.shape[1] // head_size):
        cols = slice(h * head_size, (h + 1) * head_size)
        total = functools.reduce(
            jnp.add,
            [o[:, cols].astype(jnp.float32) * w[:, h : h + 1] for o, w in zip(outs, weights)],
        )
        final[:, cols] = total.astype(final.dtype)


def merge(outs, stats, head_size):
    return pl.pallas_call(
        functools.partial(merge_kernel, head_size),
        out_shape=jax.ShapeDtypeStruct(outs[0].shape, jnp.bfloat16),
    )(*outs, *stats)


def on_device(queries, prefix_keys, cached_prefix_values, shard_len, reach, w_out):
    shard_count = lax.axis_size("blk")
    own_index = lax.axis_index("blk")
    rows, heads_local, head_size = queries.shape
    kv_local, keys_len = prefix_keys.shape[:2]
    group = heads_local // kv_local
    tile = min(1024, keys_len)
    q = queries.reshape(rows, heads_local * head_size)
    live = shard_len[own_index]

    visitors = [q] + [passed_along(q, "blk", offset) for offset in range(1, SPAN)]
    outs, stats = [], []
    for offset in range(SPAN):
        owner = (own_index - offset + shard_count) % shard_count
        bounds = jnp.stack([live, reach[owner] - offset * keys_len]).astype(jnp.int32)
        out, stat = attend(visitors[offset], prefix_keys, cached_prefix_values, bounds, group, tile)
        if offset:
            out, stat = passed_along((out, stat), "blk", -offset)
        outs.append(out)
        stats.append(stat)
    attended = merge(outs, stats, head_size)
    gathered = lax.all_gather(attended, "blk", axis=0, tiled=True)
    splits = lax.axis_size("heads")
    me = lax.axis_index("heads")
    size = gathered.shape[0] // splits

    def share(owner):
        return jnp.dot(
            lax.dynamic_slice_in_dim(gathered, owner * size, size, 0),
            w_out,
            preferred_element_type=jnp.float32,
        )

    received = []
    for step in range(1, splits):
        sent = share((me + step) % splits).astype(jnp.bfloat16)
        received.append(passed_along(sent, "heads", step))
    total = share(me)
    for piece in received:
        total = total + piece.astype(jnp.float32)
    return total.astype(jnp.bfloat16)


def solution(mesh):
    return jax.shard_map(
        on_device,
        mesh=mesh,
        in_specs=(
            P("blk", "heads", None),
            P("heads", "blk", None),
            P("heads", "blk", None),
            P(),
            P(),
            P("heads", "blk"),
        ),
        out_specs=P("heads", "blk"),
        check_vma=False,
    )
```

```python
import functools
import math

import jax
import jax.numpy as jnp
from jax import lax
from jax.experimental import pallas as pl
from jax.experimental.pallas import tpu as pltpu
from jax.sharding import PartitionSpec as P

SPAN = 4
LANES = 128
masked_score = -1e30


def passed_along(value, axis, steps):
    count = lax.axis_size(axis)
    pairs = [(source, (source + steps) % count) for source in range(count)]
    return lax.ppermute(value, axis, pairs)


def attend_kernel(tile, group, head_size, bounds, q_ref, k_ref, v_ref, o_ref, s_ref, q_all, m_ref, l_ref, acc_ref):
    rows = q_ref.shape[0]
    keys = k_ref.shape[1]
    kv = pl.program_id(0)
    live, edge = bounds[0], bounds[1]
    factor = head_size**-0.5 * math.log2(math.e)
    for g in range(group):
        q_all[g * rows : (g + 1) * rows, :] = q_ref[:, g * head_size : (g + 1) * head_size]
    m_ref[...] = jnp.full(m_ref.shape, masked_score, jnp.float32)
    l_ref[...] = jnp.zeros(l_ref.shape, jnp.float32)
    acc_ref[...] = jnp.zeros(acc_ref.shape, jnp.float32)

    def step(start, masked):
        k = k_ref[0, start : start + tile, :]
        v = v_ref[0, start : start + tile, :]
        s = lax.dot_general(
            q_all[...], k, (((1,), (1,)), ((), ())), preferred_element_type=jnp.float32
        ) * factor
        if masked:
            token = lax.broadcasted_iota(jnp.int32, (rows, tile), 0)
            slot = lax.broadcasted_iota(jnp.int32, (rows, tile), 1) + start
            seen = (slot < live) & (slot < edge + token)
            seen = jnp.concatenate([seen] * group, axis=0)
            s = jnp.where(seen, s, masked_score)
        m_old = m_ref[:, :1]
        m_new = jnp.maximum(m_old, jnp.max(s, axis=1, keepdims=True))
        p = jnp.exp2(s - m_new)
        if masked:
            p = jnp.where(seen, p, 0.0)
        shrink = jnp.exp2(m_old - m_new)
        l_new = l_ref[:, :1] * shrink + jnp.sum(p, axis=1, keepdims=True)
        acc_ref[...] = acc_ref[...] * shrink + jnp.dot(
            p.astype(jnp.bfloat16), v, preferred_element_type=jnp.float32
        )
        m_ref[...] = jnp.broadcast_to(m_new, m_ref.shape)
        l_ref[...] = jnp.broadcast_to(l_new, l_ref.shape)

    for start in range(0, keys, tile):
        whole = (start + tile <= live) & (start + tile <= edge)
        some = (start < live) & (start < edge + rows - 1)

        @pl.when(whole)
        def _():
            step(start, False)

        @pl.when(some & jnp.logical_not(whole))
        def _():
            step(start, True)

    total = l_ref[:, :1]
    held = jnp.where(total > 0.0, total, 1.0)
    out = acc_ref[...] / held
    stat = jnp.where(total > 0.0, m_ref[:, :1] + jnp.log2(held), masked_score)

    @pl.when(kv == 0)
    def _():
        s_ref[...] = jnp.full(s_ref.shape, masked_score, jnp.float32)

    lane = lax.broadcasted_iota(jnp.int32, s_ref.shape, 1)
    stats = s_ref[...]
    for g in range(group):
        o_ref[:, g * head_size : (g + 1) * head_size] = out[g * rows : (g + 1) * rows].astype(o_ref.dtype)
        stats = jnp.where(lane == kv * group + g, stat[g * rows : (g + 1) * rows], stats)
    s_ref[...] = stats


def attend(q, keys, values, bounds, group, tile):
    rows, width = q.shape
    kv_local, key_count, head_size = keys.shape
    wide = group * head_size
    return pl.pallas_call(
        functools.partial(attend_kernel, tile, group, head_size),
        out_shape=(
            jax.ShapeDtypeStruct((rows, width), jnp.bfloat16),
            jax.ShapeDtypeStruct((rows, LANES), jnp.float32),
        ),
        grid_spec=pltpu.PrefetchScalarGridSpec(
            num_scalar_prefetch=1,
            grid=(kv_local,),
            in_specs=[
                pl.BlockSpec((rows, wide), lambda i, b: (0, i)),
                pl.BlockSpec((1, key_count, head_size), lambda i, b: (i, 0, 0)),
                pl.BlockSpec((1, key_count, head_size), lambda i, b: (i, 0, 0)),
            ],
            out_specs=[
                pl.BlockSpec((rows, wide), lambda i, b: (0, i)),
                pl.BlockSpec((rows, LANES), lambda i, b: (0, 0)),
            ],
            scratch_shapes=[
                pltpu.VMEM((group * rows, head_size), jnp.bfloat16),
                pltpu.VMEM((group * rows, LANES), jnp.float32),
                pltpu.VMEM((group * rows, LANES), jnp.float32),
                pltpu.VMEM((group * rows, head_size), jnp.float32),
            ],
        ),
        compiler_params=pltpu.CompilerParams(vmem_limit_bytes=48 << 20),
        cost_estimate=pl.CostEstimate(
            flops=4 * rows * width * key_count,
            bytes_accessed=4 * rows * width + 4 * keys.size,
            transcendentals=rows * (width // head_size) * key_count,
        ),
    )(bounds, q, keys, values)


def merge_kernel(head_size, *refs):
    parts = len(refs) // 2
    outs, stats, final = refs[:parts], refs[parts : 2 * parts], refs[-1]
    joined = functools.reduce(jnp.maximum, [s[...] for s in stats])
    weights = [jnp.exp2(s[...] - joined) for s in stats]
    inverse = 1.0 / functools.reduce(jnp.add, weights)
    weights = [w * inverse for w in weights]
    for h in range(final.shape[1] // head_size):
        cols = slice(h * head_size, (h + 1) * head_size)
        total = functools.reduce(
            jnp.add,
            [o[:, cols].astype(jnp.float32) * w[:, h : h + 1] for o, w in zip(outs, weights)],
        )
        final[:, cols] = total.astype(final.dtype)


def merge(outs, stats, head_size):
    return pl.pallas_call(
        functools.partial(merge_kernel, head_size),
        out_shape=jax.ShapeDtypeStruct(outs[0].shape, jnp.bfloat16),
    )(*outs, *stats)


def project_kernel(row_sets, chunks, a_ref, w_ref, o_ref, buf, w_buf, acc, outgoing, incoming,
                   local_sem, col_send, col_recv, pair_send, pair_recv, core_send, core_recv, share_send, share_recv):
    splits = lax.axis_size("heads")
    h = lax.axis_index("heads")
    me = lax.axis_index("blk")
    r, p, c = me // 4, (me // 2) % 2, me % 2
    rows, width = a_ref.shape
    wide = width // chunks
    band = 4 * rows
    per_share = row_sets // splits
    columns = w_ref.shape[1]
    strip = min(256, columns)
    first = ((h + 1) % splits) * per_share

    def block(row_set, pair, core):
        return (row_set * 2 + pair) * 2 + core

    def view(index, chunk):
        return buf.at[chunk, pl.ds(pl.multiple_of(index * rows, rows), rows), :]

    def own(chunk):
        return a_ref.at[:, pl.ds(pl.multiple_of(chunk * wide, wide), wide)]

    def remote(src, dst, sent, landed, head, blk):
        return pltpu.make_async_remote_copy(
            src_ref=src, dst_ref=dst, send_sem=sent, recv_sem=landed,
            device_id=(head, blk), device_id_type=pl.DeviceIdType.MESH,
        )

    def to_column(d, chunk, row_set):
        return remote(own(chunk), view(block(row_set, p, c), chunk), col_send.at[(d - 1) * chunks + chunk],
                      col_recv.at[row_set * chunks + chunk], h, block((r + d) % row_sets, p, c))

    def to_pair(src, row_set, pair, chunk):
        at = row_set * chunks + chunk
        return remote(src, view(block(row_set, pair, c), chunk), pair_send.at[at], pair_recv.at[at], h, block(r, 1 - p, c))

    def to_core(src, row_set, pair, core, chunk):
        at = (pair * row_sets + row_set) * chunks + chunk
        return remote(src, view(block(row_set, pair, core), chunk), core_send.at[at], core_recv.at[at], h, block(r, p, 1 - c))

    def to_share(k):
        row_set = (first + k) % row_sets
        owner = row_set // per_share
        slot = ((h - owner + splits) % splits - 1) * per_share + row_set % per_share
        return remote(outgoing.at[k], incoming.at[slot], share_send.at[k], share_recv.at[slot], owner, me)

    def from_share(slot):
        return remote(outgoing.at[0], incoming.at[slot], share_send.at[0], share_recv.at[slot], (h + 1) % splits, me)

    barrier = pltpu.get_barrier_semaphore()
    greeted = [(h, block((r + d) % row_sets, p, c)) for d in range(1, row_sets)]
    greeted += [(h, block(r, 1 - p, c)), (h, block(r, p, 1 - c))]
    greeted += [((h + d) % splits, me) for d in range(1, splits)]
    w_copy = pltpu.make_async_copy(w_ref, w_buf, local_sem.at[chunks])
    w_copy.start()
    kept = [pltpu.make_async_copy(own(ch), view(me, ch), local_sem.at[ch]) for ch in range(chunks)]
    for copy in kept:
        copy.start()
    for peer in greeted:
        pl.semaphore_signal(barrier, inc=1, device_id=peer, device_id_type=pl.DeviceIdType.MESH)
    pl.semaphore_wait(barrier, len(greeted))

    for ch in range(chunks):
        for d in range(1, row_sets):
            to_column(d, ch, r).start()
        to_pair(own(ch), r, p, ch).start()
        to_core(own(ch), r, p, c, ch).start()
    for copy in kept:
        copy.wait()
    w_copy.wait()

    total = row_sets * chunks

    def located(t):
        k = t // chunks
        return k, t % chunks, (first + k) % row_sets

    def step(s, carry):
        @pl.when(s < total)
        def _():
            k, ch, row_set = located(s)

            @pl.when(row_set != r)
            def _():
                to_column(1, ch, row_set).wait_recv()
                to_pair(view(block(row_set, p, c), ch), row_set, p, ch).start()
                to_core(view(block(row_set, p, c), ch), row_set, p, c, ch).start()

        @pl.when((s >= 1) & (s <= total))
        def _():
            k, ch, row_set = located(s - 1)
            to_pair(view(block(row_set, 1 - p, c), ch), row_set, 1 - p, ch).wait_recv()
            to_core(view(block(row_set, 1 - p, c), ch), row_set, 1 - p, c, ch).start()

        @pl.when(s >= 2)
        def _():
            k, ch, row_set = located(s - 2)
            for pair in range(2):
                to_core(view(block(row_set, pair, 1 - c), ch), row_set, pair, 1 - c, ch).wait_recv()
            at = pl.multiple_of(row_set * band, band)

            def multiply(n, carry):
                cols = pl.ds(pl.multiple_of(n * strip, strip), strip)
                value = jnp.dot(
                    buf[ch, pl.ds(at, band), :],
                    w_buf[pl.ds(pl.multiple_of(ch * wide, wide), wide), cols],
                    preferred_element_type=jnp.float32,
                )

                @pl.when(ch == 0)
                def _():
                    acc[:, cols] = value

                @pl.when(ch > 0)
                def _():
                    acc[:, cols] += value

                return carry

            lax.fori_loop(0, columns // strip, multiply, 0)

            @pl.when((ch == chunks - 1) & (k < row_sets - per_share))
            def _():
                outgoing[k] = acc[...].astype(outgoing.dtype)
                to_share(k).start()

            @pl.when((ch == chunks - 1) & (k >= row_sets - per_share))
            def _():
                j = row_set % per_share
                value = acc[...]
                for d in range(splits - 1):
                    from_share(d * per_share + j).wait_recv()
                    value = value + incoming[d * per_share + j].astype(jnp.float32)
                o_ref[pl.ds(pl.multiple_of(j * band, band), band), :] = value.astype(o_ref.dtype)

        return carry

    lax.fori_loop(0, total + 2, step, 0)

    def drain(t, carry):
        k, ch, row_set = located(t)
        to_pair(view(me, ch), row_set, p, ch).wait_send()
        for pair in range(2):
            to_core(view(me, ch), row_set, pair, c, ch).wait_send()
        return carry

    lax.fori_loop(0, total, drain, 0)
    for ch in range(chunks):
        for d in range(1, row_sets):
            to_column(d, ch, r).wait_send()

    def drain_share(k, carry):
        to_share(k).wait_send()
        return carry

    lax.fori_loop(0, row_sets - per_share, drain_share, 0)


def project(attended, w_out, chunks):
    count, splits = lax.axis_size("blk"), lax.axis_size("heads")
    rows, width = attended.shape
    columns = w_out.shape[1]
    row_sets = count // 4
    per_share = row_sets // splits
    band = 4 * rows
    dma = pltpu.SemaphoreType.DMA
    return pl.pallas_call(
        functools.partial(project_kernel, row_sets, chunks),
        out_shape=jax.ShapeDtypeStruct((per_share * band, columns), jnp.bfloat16),
        in_specs=[pl.BlockSpec(memory_space=pl.ANY)] * 2,
        out_specs=pl.BlockSpec(memory_space=pltpu.VMEM),
        scratch_shapes=[
            pltpu.VMEM((chunks, count * rows, width // chunks), jnp.bfloat16),
            pltpu.VMEM(w_out.shape, jnp.bfloat16),
            pltpu.VMEM((band, columns), jnp.float32),
            pltpu.VMEM((row_sets - per_share, band, columns), jnp.bfloat16),
            pltpu.VMEM((row_sets - per_share, band, columns), jnp.bfloat16),
            dma((chunks + 1,)),
            dma(((row_sets - 1) * chunks,)),
            dma((row_sets * chunks,)),
            dma((row_sets * chunks,)),
            dma((row_sets * chunks,)),
            dma((2 * row_sets * chunks,)),
            dma((2 * row_sets * chunks,)),
            dma((row_sets - per_share,)),
            dma((row_sets - per_share,)),
        ],
        compiler_params=pltpu.CompilerParams(
            collective_id=0, has_side_effects=True, vmem_limit_bytes=48 << 20
        ),
    )(attended, w_out)


def on_device(queries, prefix_keys, cached_prefix_values, shard_len, reach, w_out):
    shard_count = lax.axis_size("blk")
    own_index = lax.axis_index("blk")
    rows, heads_local, head_size = queries.shape
    kv_local, keys_len = prefix_keys.shape[:2]
    group = heads_local // kv_local
    tile = min(1024, keys_len)
    q = queries.reshape(rows, heads_local * head_size)
    live = shard_len[own_index]

    visitors = [q] + [passed_along(q, "blk", offset) for offset in range(1, SPAN)]
    outs, stats = [], []
    for offset in range(SPAN):
        owner = (own_index - offset + shard_count) % shard_count
        bounds = jnp.stack([live, reach[owner] - offset * keys_len]).astype(jnp.int32)
        out, stat = attend(visitors[offset], prefix_keys, cached_prefix_values, bounds, group, tile)
        if offset:
            out, stat = passed_along((out, stat), "blk", -offset)
        outs.append(out)
        stats.append(stat)
    attended = merge(outs, stats, head_size)
    return project(attended, w_out, 2)


def solution(mesh):
    return jax.shard_map(
        on_device,
        mesh=mesh,
        in_specs=(
            P("blk", "heads", None),
            P("heads", "blk", None),
            P("heads", "blk", None),
            P(),
            P(),
            P("heads", "blk"),
        ),
        out_specs=P("heads", "blk"),
        check_vma=False,
    )
```

```python
import functools
import math

import jax
import jax.numpy as jnp
from jax import lax
from jax.experimental import pallas as pl
from jax.experimental.pallas import tpu as pltpu
from jax.sharding import PartitionSpec as P

SPAN = 4
masked_score = -1e30


def layer_kernel(row_sets, chunks, rows, q_ref, k_ref, v_ref, live_ref, reach_ref, w_ref, o_ref,
                 q_all, k_all, v_all, part_own, stat_own, part_out, stat_out, part_in, stat_in,
                 buf, w_buf, acc, outgoing, incoming,
                 local_sem, q_send, q_recv, part_send, part_recv, stat_send, stat_recv,
                 col_send, col_recv, pair_send, pair_recv, core_send, core_recv, share_send, share_recv):
    splits = lax.axis_size("heads")
    count = lax.axis_size("blk")
    h = lax.axis_index("heads")
    me = lax.axis_index("blk")
    r, p, c = me // 4, (me // 2) % 2, me % 2
    kv_local, lanes, head_size = q_ref.shape
    group = lanes // rows
    keys = k_ref.shape[1]
    per_chunk = kv_local // chunks
    wide = per_chunk * group * head_size
    band = 4 * rows
    per_share = row_sets // splits
    columns = w_ref.shape[1]
    strip = min(256, columns)
    first = ((h + 1) % splits) * per_share
    visits = SPAN - 1

    def block(row_set, pair, core):
        return (row_set * 2 + pair) * 2 + core

    def view(index, chunk):
        return buf.at[chunk, pl.ds(pl.multiple_of(index * rows, rows), rows), :]

    def remote(src, dst, sent, landed, head, blk):
        return pltpu.make_async_remote_copy(
            src_ref=src, dst_ref=dst, send_sem=sent, recv_sem=landed,
            device_id=(head, blk), device_id_type=pl.DeviceIdType.MESH,
        )

    def heads_of(chunk):
        return pl.ds(chunk * per_chunk, per_chunk)

    def to_visit(offset, chunk):
        at = (offset - 1) * chunks + chunk
        return remote(q_ref.at[heads_of(chunk)], q_all.at[offset, heads_of(chunk)], q_send.at[at], q_recv.at[at],
                      h, (me + offset) % count)

    def part_home(offset, chunk):
        at = (offset - 1) * chunks + chunk
        return remote(part_out.at[offset - 1, heads_of(chunk)], part_in.at[offset - 1, heads_of(chunk)],
                      part_send.at[at], part_recv.at[at], h, (me - offset + count) % count)

    def stat_home(offset, chunk):
        at = (offset - 1) * chunks + chunk
        return remote(stat_out.at[offset - 1, heads_of(chunk)], stat_in.at[offset - 1, heads_of(chunk)],
                      stat_send.at[at], stat_recv.at[at], h, (me - offset + count) % count)

    def to_column(d, chunk, row_set):
        return remote(view(me, chunk), view(block(row_set, p, c), chunk), col_send.at[(d - 1) * chunks + chunk],
                      col_recv.at[row_set * chunks + chunk], h, block((r + d) % row_sets, p, c))

    def to_pair(row_set, pair, chunk):
        at = row_set * chunks + chunk
        spot = view(block(row_set, pair, c), chunk)
        return remote(spot, spot, pair_send.at[at], pair_recv.at[at], h, block(r, 1 - p, c))

    def to_core(row_set, pair, core, chunk):
        at = (pair * row_sets + row_set) * chunks + chunk
        spot = view(block(row_set, pair, core), chunk)
        return remote(spot, spot, core_send.at[at], core_recv.at[at], h, block(r, p, 1 - c))

    def to_share(k):
        row_set = (first + k) % row_sets
        owner = row_set // per_share
        slot = ((h - owner + splits) % splits - 1) * per_share + row_set % per_share
        return remote(outgoing.at[k], incoming.at[slot], share_send.at[k], share_recv.at[slot], owner, me)

    def from_share(slot):
        return remote(outgoing.at[0], incoming.at[slot], share_send.at[0], share_recv.at[slot], (h + 1) % splits, me)

    q_copy = pltpu.make_async_copy(q_ref, q_all.at[0], local_sem.at[0])
    k_copy = pltpu.make_async_copy(k_ref, k_all, local_sem.at[1])
    v_copy = pltpu.make_async_copy(v_ref, v_all, local_sem.at[2])
    w_copy = pltpu.make_async_copy(w_ref, w_buf, local_sem.at[3])
    for copy in (q_copy, k_copy, v_copy, w_copy):
        copy.start()
    greeted = [(h, block((r + d) % row_sets, p, c)) for d in range(1, row_sets)]
    greeted += [(h, block(r, 1 - p, c)), (h, block(r, p, 1 - c))]
    greeted += [((h + d) % splits, me) for d in range(1, splits)]
    for d in range(1, SPAN):
        greeted += [(h, (me + d) % count), (h, (me - d + count) % count)]
    barrier = pltpu.get_barrier_semaphore()
    for peer in greeted:
        pl.semaphore_signal(barrier, inc=1, device_id=peer, device_id_type=pl.DeviceIdType.MESH)
    pl.semaphore_wait(barrier, len(greeted))
    for ch in range(chunks):
        for offset in range(1, SPAN):
            to_visit(offset, ch).start()
    q_copy.wait()
    k_copy.wait()
    v_copy.wait()

    live = live_ref[me]
    factor = head_size**-0.5 * math.log2(math.e)
    sub = min(256, lanes)

    def attend(offset, chunk):
        edge = reach_ref[(me - offset + count) % count] - offset * keys
        token = lax.broadcasted_iota(jnp.int32, (1, sub), 1) % rows
        limit = jnp.minimum(edge + token, live)
        slot = lax.broadcasted_iota(jnp.int32, (keys, sub), 0)
        seen = slot < limit

        def one(i, carry):
            kv = chunk * per_chunk + i
            key_tile, value_tile = k_all[kv], v_all[kv]
            for start in range(0, lanes, sub):
                cols = slice(start, start + sub)
                s = lax.dot_general(
                    key_tile, q_all[offset, kv, cols, :], (((1,), (1,)), ((), ())),
                    preferred_element_type=jnp.float32,
                )
                s = jnp.where(seen, s * factor, masked_score)
                m = jnp.max(s, axis=0, keepdims=True)
                weight = jnp.exp2(s - m)
                total = jnp.sum(weight, axis=0, keepdims=True)
                part = lax.dot_general(
                    value_tile, weight.astype(jnp.bfloat16), (((0,), (0,)), ((), ())),
                    preferred_element_type=jnp.float32,
                )
                part = (part * (1.0 / total)).astype(jnp.bfloat16)
                stat = jnp.broadcast_to(m + jnp.log2(total), (8, sub))

                @pl.when(offset == 0)
                def _():
                    part_own[kv, :, cols] = part
                    stat_own[kv, :, cols] = stat

                @pl.when(offset > 0)
                def _():
                    part_out[offset - 1, kv, :, cols] = part
                    stat_out[offset - 1, kv, :, cols] = stat

            return carry

        lax.fori_loop(0, per_chunk, one, 0)

    def merge(chunk):
        for offset in range(1, SPAN):
            part_home(offset, chunk).wait_recv()
            stat_home(offset, chunk).wait_recv()
        spot = pl.ds(pl.multiple_of(me * rows, rows), rows)
        for i in range(per_chunk):
            kv = chunk * per_chunk + i
            stats = [stat_own[kv, :1, :]] + [stat_in[j, kv, :1, :] for j in range(visits)]
            joined = functools.reduce(jnp.maximum, stats)
            weights = [jnp.exp2(s - joined) for s in stats]
            inverse = 1.0 / functools.reduce(jnp.add, weights)
            parts = [part_own[kv]] + [part_in[j, kv] for j in range(visits)]
            total = functools.reduce(
                jnp.add, [x.astype(jnp.float32) * (w * inverse) for x, w in zip(parts, weights)]
            )
            total = total.T.astype(jnp.bfloat16)
            for g in range(group):
                at = (i * group + g) * head_size
                buf[chunk, spot, at : at + head_size] = total[g * rows : (g + 1) * rows]
        for d in range(1, row_sets):
            to_column(d, chunk, r).start()
        to_pair(r, p, chunk).start()
        to_core(r, p, c, chunk).start()

    def relay(row_set, chunk):
        @pl.when(row_set != r)
        def _():
            to_column(1, chunk, row_set).wait_recv()
            to_pair(row_set, p, chunk).start()
            to_core(row_set, p, c, chunk).start()

    def unit(u, carry):
        early = u < chunks
        offset = jnp.where(early, 0, (u - chunks) % visits + 1)
        chunk = jnp.where(early, u, (u - chunks) // visits)

        @pl.when(offset > 0)
        def _():
            to_visit(offset, chunk).wait_recv()

        attend(offset, chunk)

        @pl.when(offset > 0)
        def _():
            part_home(offset, chunk).start()
            stat_home(offset, chunk).start()

        for ch in range(chunks - 1):
            @pl.when(u == chunks + visits * (ch + 1))
            def _():
                merge(ch)

        return carry

    lax.fori_loop(0, SPAN * chunks, unit, 0)

    def relay_early(t, carry):
        relay((first + t % row_sets) % row_sets, t // row_sets)
        return carry

    lax.fori_loop(0, row_sets * (chunks - 1), relay_early, 0)
    merge(chunks - 1)
    w_copy.wait()

    total = row_sets * chunks

    def located(t):
        k = t % row_sets
        return k, t // row_sets, (first + k) % row_sets

    def step(s, carry):
        @pl.when((s < total) & (s >= total - row_sets))
        def _():
            k, ch, row_set = located(s)
            relay(row_set, ch)

        @pl.when((s >= 1) & (s <= total))
        def _():
            k, ch, row_set = located(s - 1)
            to_pair(row_set, 1 - p, ch).wait_recv()
            to_core(row_set, 1 - p, c, ch).start()

        @pl.when(s >= 2)
        def _():
            k, ch, row_set = located(s - 2)
            for pair in range(2):
                to_core(row_set, pair, 1 - c, ch).wait_recv()
            at = pl.multiple_of(row_set * band, band)

            def multiply(n, carry):
                cols = pl.ds(pl.multiple_of(n * strip, strip), strip)
                value = jnp.dot(
                    buf[ch, pl.ds(at, band), :],
                    w_buf[pl.ds(pl.multiple_of(ch * wide, wide), wide), cols],
                    preferred_element_type=jnp.float32,
                )

                @pl.when(ch == 0)
                def _():
                    acc[k, :, cols] = value

                @pl.when(ch > 0)
                def _():
                    acc[k, :, cols] += value

                return carry

            lax.fori_loop(0, columns // strip, multiply, 0)

            @pl.when((ch == chunks - 1) & (k < row_sets - per_share))
            def _():
                outgoing[k] = acc[k].astype(outgoing.dtype)
                to_share(k).start()

            @pl.when((ch == chunks - 1) & (k >= row_sets - per_share))
            def _():
                j = row_set % per_share
                value = acc[k]
                for d in range(splits - 1):
                    from_share(d * per_share + j).wait_recv()
                    value = value + incoming[d * per_share + j].astype(jnp.float32)
                o_ref[pl.ds(pl.multiple_of(j * band, band), band), :] = value.astype(o_ref.dtype)

        return carry

    lax.fori_loop(0, total + 2, step, 0)

    for ch in range(chunks):
        for offset in range(1, SPAN):
            to_visit(offset, ch).wait_send()
            part_home(offset, ch).wait_send()
            stat_home(offset, ch).wait_send()
        for d in range(1, row_sets):
            to_column(d, ch, r).wait_send()

    def drain(t, carry):
        k, ch, row_set = located(t)
        to_pair(row_set, p, ch).wait_send()
        for pair in range(2):
            to_core(row_set, pair, c, ch).wait_send()
        return carry

    lax.fori_loop(0, total, drain, 0)

    def drain_share(k, carry):
        to_share(k).wait_send()
        return carry

    lax.fori_loop(0, row_sets - per_share, drain_share, 0)


def on_device(queries, prefix_keys, cached_prefix_values, shard_len, reach, w_out):
    count, splits = lax.axis_size("blk"), lax.axis_size("heads")
    rows, heads_local, head_size = queries.shape
    kv_local, keys_len = prefix_keys.shape[:2]
    group = heads_local // kv_local
    lanes = group * rows
    chunks = 2 if kv_local % 2 == 0 else 1
    columns = w_out.shape[1]
    row_sets = count // 4
    per_share = row_sets // splits
    band = 4 * rows
    visits = SPAN - 1
    q = queries.reshape(rows, kv_local, group, head_size).transpose(1, 2, 0, 3).reshape(kv_local, lanes, head_size)
    dma = pltpu.SemaphoreType.DMA
    bf16, f32 = jnp.bfloat16, jnp.float32
    anywhere = pl.BlockSpec(memory_space=pl.ANY)
    scalars = pl.BlockSpec(memory_space=pltpu.SMEM)
    each = dma((visits * chunks,))
    sets = dma((row_sets * chunks,))
    return pl.pallas_call(
        functools.partial(layer_kernel, row_sets, chunks, rows),
        out_shape=jax.ShapeDtypeStruct((per_share * band, columns), bf16),
        in_specs=[anywhere, anywhere, anywhere, scalars, scalars, anywhere],
        out_specs=pl.BlockSpec(memory_space=pltpu.VMEM),
        scratch_shapes=[
            pltpu.VMEM((SPAN, kv_local, lanes, head_size), bf16),
            pltpu.VMEM(prefix_keys.shape, bf16),
            pltpu.VMEM(prefix_keys.shape, bf16),
            pltpu.VMEM((kv_local, head_size, lanes), bf16),
            pltpu.VMEM((kv_local, 8, lanes), f32),
            pltpu.VMEM((visits, kv_local, head_size, lanes), bf16),
            pltpu.VMEM((visits, kv_local, 8, lanes), f32),
            pltpu.VMEM((visits, kv_local, head_size, lanes), bf16),
            pltpu.VMEM((visits, kv_local, 8, lanes), f32),
            pltpu.VMEM((chunks, count * rows, heads_local * head_size // chunks), bf16),
            pltpu.VMEM(w_out.shape, bf16),
            pltpu.VMEM((row_sets, band, columns), f32),
            pltpu.VMEM((row_sets - per_share, band, columns), bf16),
            pltpu.VMEM((row_sets - per_share, band, columns), bf16),
            dma((4,)),
            each, each, each, each, each, each,
            dma(((row_sets - 1) * chunks,)),
            sets, sets, sets,
            dma((2 * row_sets * chunks,)),
            dma((2 * row_sets * chunks,)),
            dma((row_sets - per_share,)),
            dma((row_sets - per_share,)),
        ],
        compiler_params=pltpu.CompilerParams(
            collective_id=0, has_side_effects=True, vmem_limit_bytes=60 << 20
        ),
    )(q, prefix_keys, cached_prefix_values, shard_len, reach, w_out)


def solution(mesh):
    return jax.shard_map(
        on_device,
        mesh=mesh,
        in_specs=(
            P("blk", "heads", None),
            P("heads", "blk", None),
            P("heads", "blk", None),
            P(),
            P(),
            P("heads", "blk"),
        ),
        out_specs=P("heads", "blk"),
        check_vma=False,
    )
```

```python
import functools
import math

import jax
import jax.numpy as jnp
from jax import lax
from jax.experimental import pallas as pl
from jax.experimental.pallas import tpu as pltpu
from jax.sharding import PartitionSpec as P

SPAN = 4
masked_score = -1e30


def layer_kernel(row_sets, chunks, rows, q_ref, k_ref, v_ref, live_ref, reach_ref, w_ref, o_ref,
                 q_all, k_all, v_all, part_own, stat_own, part_out, stat_out, part_in, stat_in,
                 buf, w_buf, acc, outgoing, incoming,
                 local_sem, q_send, q_recv, part_send, part_recv, stat_send, stat_recv,
                 col_send, col_recv, pair_send, pair_recv, core_send, core_recv, share_send, share_recv):
    splits = lax.axis_size("heads")
    count = lax.axis_size("blk")
    h = lax.axis_index("heads")
    me = lax.axis_index("blk")
    r, p, c = me // 4, (me // 2) % 2, me % 2
    kv_local, lanes, head_size = q_ref.shape
    group = lanes // rows
    keys = k_ref.shape[1]
    per_chunk = kv_local // chunks
    wide = per_chunk * group * head_size
    band = 4 * rows
    per_share = row_sets // splits
    columns = w_ref.shape[1]
    strip = min(256, columns)
    first = ((h + 1) % splits) * per_share
    visits = SPAN - 1

    def block(row_set, pair, core):
        return (row_set * 2 + pair) * 2 + core

    def view(index, chunk):
        return buf.at[chunk, pl.ds(pl.multiple_of(index * rows, rows), rows), :]

    def remote(src, dst, sent, landed, head, blk):
        return pltpu.make_async_remote_copy(
            src_ref=src, dst_ref=dst, send_sem=sent, recv_sem=landed,
            device_id=(head, blk), device_id_type=pl.DeviceIdType.MESH,
        )

    def heads_of(chunk):
        return pl.ds(chunk * per_chunk, per_chunk)

    def to_visit(offset, chunk):
        at = (offset - 1) * chunks + chunk
        return remote(q_ref.at[heads_of(chunk)], q_all.at[offset, heads_of(chunk)], q_send.at[at], q_recv.at[at],
                      h, (me + offset) % count)

    def part_home(offset, chunk):
        at = (offset - 1) * chunks + chunk
        return remote(part_out.at[offset - 1, heads_of(chunk)], part_in.at[offset - 1, heads_of(chunk)],
                      part_send.at[at], part_recv.at[at], h, (me - offset + count) % count)

    def stat_home(offset, chunk):
        at = (offset - 1) * chunks + chunk
        return remote(stat_out.at[offset - 1, heads_of(chunk)], stat_in.at[offset - 1, heads_of(chunk)],
                      stat_send.at[at], stat_recv.at[at], h, (me - offset + count) % count)

    def to_column(d, chunk, row_set):
        return remote(view(me, chunk), view(block(row_set, p, c), chunk), col_send.at[(d - 1) * chunks + chunk],
                      col_recv.at[row_set * chunks + chunk], h, block((r + d) % row_sets, p, c))

    def to_pair(row_set, pair, chunk):
        at = row_set * chunks + chunk
        spot = view(block(row_set, pair, c), chunk)
        return remote(spot, spot, pair_send.at[at], pair_recv.at[at], h, block(r, 1 - p, c))

    def to_core(row_set, pair, core, chunk):
        at = (pair * row_sets + row_set) * chunks + chunk
        spot = view(block(row_set, pair, core), chunk)
        return remote(spot, spot, core_send.at[at], core_recv.at[at], h, block(r, p, 1 - c))

    def to_share(k):
        row_set = (first + k) % row_sets
        owner = row_set // per_share
        slot = ((h - owner + splits) % splits - 1) * per_share + row_set % per_share
        return remote(outgoing.at[k], incoming.at[slot], share_send.at[k], share_recv.at[slot], owner, me)

    def from_share(slot):
        return remote(outgoing.at[0], incoming.at[slot], share_send.at[0], share_recv.at[slot], (h + 1) % splits, me)

    q_copy = pltpu.make_async_copy(q_ref, q_all.at[0], local_sem.at[0])
    k_copy = pltpu.make_async_copy(k_ref, k_all, local_sem.at[1])
    v_copy = pltpu.make_async_copy(v_ref, v_all, local_sem.at[2])
    w_copy = pltpu.make_async_copy(w_ref, w_buf, local_sem.at[3])
    for copy in (q_copy, k_copy, v_copy, w_copy):
        copy.start()
    greeted = [(h, block((r + d) % row_sets, p, c)) for d in range(1, row_sets)]
    greeted += [(h, block(r, 1 - p, c)), (h, block(r, p, 1 - c))]
    greeted += [((h + d) % splits, me) for d in range(1, splits)]
    for d in range(1, SPAN):
        greeted += [(h, (me + d) % count), (h, (me - d + count) % count)]
    barrier = pltpu.get_barrier_semaphore()
    for peer in greeted:
        pl.semaphore_signal(barrier, inc=1, device_id=peer, device_id_type=pl.DeviceIdType.MESH)
    pl.semaphore_wait(barrier, len(greeted))
    for ch in range(chunks):
        for offset in range(1, SPAN):
            to_visit(offset, ch).start()
    q_copy.wait()
    k_copy.wait()
    v_copy.wait()

    live = live_ref[me]
    factor = head_size**-0.5 * math.log2(math.e)
    sub = min(512, lanes)

    def attend(offset, chunk):
        edge = reach_ref[(me - offset + count) % count] - offset * keys
        token = lax.broadcasted_iota(jnp.int32, (1, sub), 1) % rows
        limit = jnp.minimum(edge + token, live)
        slot = lax.broadcasted_iota(jnp.int32, (keys, sub), 0)
        seen = slot < limit

        def one(i, carry):
            kv = chunk * per_chunk + i
            key_tile, value_tile = k_all[kv], v_all[kv]
            for start in range(0, lanes, sub):
                cols = slice(start, start + sub)
                s = lax.dot_general(
                    key_tile, q_all[offset, kv, cols, :], (((1,), (1,)), ((), ())),
                    preferred_element_type=jnp.float32,
                )
                s = jnp.where(seen, s * factor, masked_score)
                m = jnp.max(s, axis=0, keepdims=True)
                weight = jnp.exp2(s - m)
                total = jnp.sum(weight, axis=0, keepdims=True)
                part = lax.dot_general(
                    value_tile, weight.astype(jnp.bfloat16), (((0,), (0,)), ((), ())),
                    preferred_element_type=jnp.float32,
                )
                part = (part * (1.0 / total)).astype(jnp.bfloat16)
                stat = jnp.broadcast_to(m + jnp.log2(total), (8, sub))

                @pl.when(offset == 0)
                def _():
                    part_own[kv, :, cols] = part
                    stat_own[kv, :, cols] = stat

                @pl.when(offset > 0)
                def _():
                    part_out[offset - 1, kv, :, cols] = part
                    stat_out[offset - 1, kv, :, cols] = stat

            return carry

        lax.fori_loop(0, per_chunk, one, 0)

    def merge(chunk):
        for offset in range(1, SPAN):
            part_home(offset, chunk).wait_recv()
            stat_home(offset, chunk).wait_recv()
        spot = pl.ds(pl.multiple_of(me * rows, rows), rows)
        for i in range(per_chunk):
            kv = chunk * per_chunk + i
            stats = [stat_own[kv, :1, :]] + [stat_in[j, kv, :1, :] for j in range(visits)]
            joined = functools.reduce(jnp.maximum, stats)
            weights = [jnp.exp2(s - joined) for s in stats]
            inverse = 1.0 / functools.reduce(jnp.add, weights)
            parts = [part_own[kv]] + [part_in[j, kv] for j in range(visits)]
            total = functools.reduce(
                jnp.add, [x.astype(jnp.float32) * (w * inverse) for x, w in zip(parts, weights)]
            )
            total = total.T.astype(jnp.bfloat16)
            for g in range(group):
                at = (i * group + g) * head_size
                buf[chunk, spot, at : at + head_size] = total[g * rows : (g + 1) * rows]
        for d in range(1, row_sets):
            to_column(d, chunk, r).start()
        to_pair(r, p, chunk).start()
        to_core(r, p, c, chunk).start()

    def relay(row_set, chunk):
        @pl.when(row_set != r)
        def _():
            to_column(1, chunk, row_set).wait_recv()
            to_pair(row_set, p, chunk).start()
            to_core(row_set, p, c, chunk).start()

    def unit(u, carry):
        early = u < chunks
        offset = jnp.where(early, 0, (u - chunks) % visits + 1)
        chunk = jnp.where(early, u, (u - chunks) // visits)

        @pl.when(offset > 0)
        def _():
            to_visit(offset, chunk).wait_recv()

        attend(offset, chunk)

        @pl.when(offset > 0)
        def _():
            part_home(offset, chunk).start()
            stat_home(offset, chunk).start()

        for ch in range(chunks - 1):
            @pl.when(u == chunks + visits * (ch + 1))
            def _():
                merge(ch)

        return carry

    lax.fori_loop(0, SPAN * chunks, unit, 0)

    def relay_early(t, carry):
        relay((first + t % row_sets) % row_sets, t // row_sets)
        return carry

    lax.fori_loop(0, row_sets * (chunks - 1), relay_early, 0)
    merge(chunks - 1)
    w_copy.wait()

    total = row_sets * chunks

    def located(t):
        k = t % row_sets
        return k, t // row_sets, (first + k) % row_sets

    def step(s, carry):
        @pl.when((s < total) & (s >= total - row_sets))
        def _():
            k, ch, row_set = located(s)
            relay(row_set, ch)

        @pl.when((s >= 1) & (s <= total))
        def _():
            k, ch, row_set = located(s - 1)
            to_pair(row_set, 1 - p, ch).wait_recv()
            to_core(row_set, 1 - p, c, ch).start()

        @pl.when(s >= 2)
        def _():
            k, ch, row_set = located(s - 2)
            for pair in range(2):
                to_core(row_set, pair, 1 - c, ch).wait_recv()
            at = pl.multiple_of(row_set * band, band)

            def multiply(n, carry):
                cols = pl.ds(pl.multiple_of(n * strip, strip), strip)
                value = jnp.dot(
                    buf[ch, pl.ds(at, band), :],
                    w_buf[pl.ds(pl.multiple_of(ch * wide, wide), wide), cols],
                    preferred_element_type=jnp.float32,
                )

                @pl.when(ch == 0)
                def _():
                    acc[k, :, cols] = value

                @pl.when(ch > 0)
                def _():
                    acc[k, :, cols] += value

                return carry

            lax.fori_loop(0, columns // strip, multiply, 0)

            @pl.when((ch == chunks - 1) & (k < row_sets - per_share))
            def _():
                outgoing[k] = acc[k].astype(outgoing.dtype)
                to_share(k).start()

            @pl.when((ch == chunks - 1) & (k >= row_sets - per_share))
            def _():
                j = row_set % per_share
                value = acc[k]
                for d in range(splits - 1):
                    from_share(d * per_share + j).wait_recv()
                    value = value + incoming[d * per_share + j].astype(jnp.float32)
                o_ref[pl.ds(pl.multiple_of(j * band, band), band), :] = value.astype(o_ref.dtype)

        return carry

    lax.fori_loop(0, total + 2, step, 0)

    for ch in range(chunks):
        for offset in range(1, SPAN):
            to_visit(offset, ch).wait_send()
            part_home(offset, ch).wait_send()
            stat_home(offset, ch).wait_send()
        for d in range(1, row_sets):
            to_column(d, ch, r).wait_send()

    def drain(t, carry):
        k, ch, row_set = located(t)
        to_pair(row_set, p, ch).wait_send()
        for pair in range(2):
            to_core(row_set, pair, c, ch).wait_send()
        return carry

    lax.fori_loop(0, total, drain, 0)

    def drain_share(k, carry):
        to_share(k).wait_send()
        return carry

    lax.fori_loop(0, row_sets - per_share, drain_share, 0)


def on_device(queries, prefix_keys, cached_prefix_values, shard_len, reach, w_out):
    count, splits = lax.axis_size("blk"), lax.axis_size("heads")
    rows, heads_local, head_size = queries.shape
    kv_local, keys_len = prefix_keys.shape[:2]
    group = heads_local // kv_local
    lanes = group * rows
    chunks = 2 if kv_local % 2 == 0 else 1
    columns = w_out.shape[1]
    row_sets = count // 4
    per_share = row_sets // splits
    band = 4 * rows
    visits = SPAN - 1
    q = queries.reshape(rows, kv_local, group, head_size).transpose(1, 2, 0, 3).reshape(kv_local, lanes, head_size)
    dma = pltpu.SemaphoreType.DMA
    bf16, f32 = jnp.bfloat16, jnp.float32
    anywhere = pl.BlockSpec(memory_space=pl.ANY)
    scalars = pl.BlockSpec(memory_space=pltpu.SMEM)
    each = dma((visits * chunks,))
    sets = dma((row_sets * chunks,))
    return pl.pallas_call(
        functools.partial(layer_kernel, row_sets, chunks, rows),
        out_shape=jax.ShapeDtypeStruct((per_share * band, columns), bf16),
        in_specs=[anywhere, anywhere, anywhere, scalars, scalars, anywhere],
        out_specs=pl.BlockSpec(memory_space=pltpu.VMEM),
        scratch_shapes=[
            pltpu.VMEM((SPAN, kv_local, lanes, head_size), bf16),
            pltpu.VMEM(prefix_keys.shape, bf16),
            pltpu.VMEM(prefix_keys.shape, bf16),
            pltpu.VMEM((kv_local, head_size, lanes), bf16),
            pltpu.VMEM((kv_local, 8, lanes), f32),
            pltpu.VMEM((visits, kv_local, head_size, lanes), bf16),
            pltpu.VMEM((visits, kv_local, 8, lanes), f32),
            pltpu.VMEM((visits, kv_local, head_size, lanes), bf16),
            pltpu.VMEM((visits, kv_local, 8, lanes), f32),
            pltpu.VMEM((chunks, count * rows, heads_local * head_size // chunks), bf16),
            pltpu.VMEM(w_out.shape, bf16),
            pltpu.VMEM((row_sets, band, columns), f32),
            pltpu.VMEM((row_sets - per_share, band, columns), bf16),
            pltpu.VMEM((row_sets - per_share, band, columns), bf16),
            dma((4,)),
            each, each, each, each, each, each,
            dma(((row_sets - 1) * chunks,)),
            sets, sets, sets,
            dma((2 * row_sets * chunks,)),
            dma((2 * row_sets * chunks,)),
            dma((row_sets - per_share,)),
            dma((row_sets - per_share,)),
        ],
        compiler_params=pltpu.CompilerParams(
            collective_id=0, has_side_effects=True, vmem_limit_bytes=60 << 20
        ),
    )(q, prefix_keys, cached_prefix_values, shard_len, reach, w_out)


def solution(mesh):
    return jax.shard_map(
        on_device,
        mesh=mesh,
        in_specs=(
            P("blk", "heads", None),
            P("heads", "blk", None),
            P("heads", "blk", None),
            P(),
            P(),
            P("heads", "blk"),
        ),
        out_specs=P("heads", "blk"),
        check_vma=False,
    )
```
